256 devices in a mesh: sub: 64 (over x, z, core), slab: 4 (over y).
Axes of the slice: x: 4, y: 4, z: 8, core: 2. Of those that a mesh axis runs over, the one named last changes fastest.
Arguments:
- adjoint_load: float32 [4, 64, 2, 4, 3200], P('slab', 'sub')
- design: float32 [4, 64, 2032], P('slab', 'sub'), may hold values from 0 to 1
- viscous_block: float32 [24, 24], replicated
- brinkman_block: float32 [24, 24], replicated
- coupling: float32 [8, 24], replicated, may hold values from -1.2 to 1.2
- stabilization: float32 [8, 8], replicated
- neighbours: int32 [4, 64, 3], P('slab', 'sub'), may hold values from -1 to 63, as said below
- iface_nodes: int32 [4, 64, 3, 256], P('slab', 'sub'), may hold values from 0 to 3199, as said below
- iface_count: int32 [4, 64, 3], P('slab', 'sub'), may hold values from 0 to 256, as said below
- face_nodes: int32 [4, 64, 2, 512], P('slab', 'sub'), may hold values from 0 to 3199, as said below
- owner_ids: int32 [4, 64, 3, 256], P('slab', 'sub'), may hold values from 0 to 63, as said below
Outputs:
- solution: float32 [4, 64, 2, 4, 3200], P('slab', 'sub')
- coefficients: float32 [2, 3], replicated
The draws below stay inside these ranges and needn't reach their ends.
Inputs may be any that keep to these rules, and one draw needn't show every extreme that they name: In round r the neighbour of subdomain i is i XOR 2^r or -1 for none; two neighbours list each other. `iface_nodes`: per subdomain, all entries here and in face_nodes are distinct local nodes. Slot k of round r names the same physical node on a subdomain and on its round-r neighbour; only the first iface_count slots are shared. `iface_count`: equal on both sides of a pair, 0 where the round has no neighbour. `face_nodes`: face 0 is the lower face, face 1 the upper one; slot k of the upper face of slab s is slot k of the lower face of slab s + 1 at the same index along sub. `owner_ids`: for a used slot, one of the two subdomains of the pair, the same on both sides; for an unused slot, the subdomain's own index.
All inputs are finite; a program needn't handle non-finite values.
Results may differ from the reference program's by a relative error of at most 0.0003.
Values sent between devices are 32-bit elements; how exact they have to be, the bound alone decides.
No kernel may reach another device: no remote copies, remote signals or barrier semaphores. Data moves between devices by JAX's collectives and lax.ppermute only.
A program may use at most 128 MiB of HBM per device.

```python
import functools
from functools import partial
import jax
import jax.numpy as jnp
from jax import lax

EX = 4
EY = 4
EZ = 127
IFACE = 256
FACE = 512
ROUNDS = 3
KRYLOV = 3
CASES = 2
SUBS = 64
SLABS = 4
ELEMS = 2032
NODES = 3200


def draw_adjoint_load(key, part):
    extent = (SLABS, SUBS, CASES, 4, NODES)
    device_order = (jnp.arange(SLABS)[:, None] * SUBS + jnp.arange(SUBS)[None, :]).astype(jnp.float32)
    rising = (1.0 + 2.0 * device_order / (SLABS * SUBS - 1))[:, :, None, None, None]
    noise = jax.random.normal(key, extent, jnp.float32)
    return (rising * jnp.clip(noise, -4.0, 4.0)).astype(jnp.float32)


def dominant(key, extent, spread, leading_base):
    key_spread, key_leading = jax.random.split(key)
    spread_part = jax.random.uniform(key_spread, (extent, extent), jnp.float32, -spread, spread)
    leading = leading_base + jax.random.uniform(key_leading, (extent,), jnp.float32, 0.0, 1.0)
    identity = jnp.eye(extent, dtype=jnp.float32)
    return (spread_part * (1.0 - identity) + identity * leading[:, None]).astype(jnp.float32)


def draw_viscous_block(key, part):
    return dominant(jax.random.fold_in(key, 1), 24, 0.7, 2.5)


def draw_brinkman_block(key, part):
    return dominant(jax.random.fold_in(key, 2), 24, 0.15, 1.0)


def draw_stabilization(key, part):
    return dominant(jax.random.fold_in(key, 3), 8, 0.5, 1.0)


def swap_values(order, first_value, second_value):
    return jnp.where(order == first_value, second_value, jnp.where(order == second_value, first_value, order))


def place_ends(order, device_id):
    top_value = NODES - 1
    face_start = ROUNDS * IFACE
    even = device_id % 2 == 0
    head_value = jnp.where(even, top_value, 0).astype(jnp.int32)
    face_value = jnp.where(even, 0, top_value).astype(jnp.int32)
    order = swap_values(order, order[0], head_value)
    order = swap_values(order, order[face_start], face_value)
    return order


def subdomain_layout(key):
    stream = jax.random.fold_in(key, 11)
    device_keys = jax.random.split(stream, SLABS * SUBS)
    orders = jax.vmap(functools.partial(jax.random.permutation, x=NODES))(device_keys).astype(jnp.int32)
    device_ids = jnp.arange(SLABS * SUBS, dtype=jnp.int32)
    return jax.vmap(place_ends)(orders, device_ids).astype(jnp.int32)


def draw_iface_nodes(key, part):
    orders = subdomain_layout(key)
    return orders[:, :ROUNDS * IFACE].reshape(SLABS, SUBS, ROUNDS, IFACE)


def draw_face_nodes(key, part):
    orders = subdomain_layout(key)
    return orders[:, ROUNDS * IFACE:ROUNDS * IFACE + 2 * FACE].reshape(SLABS, SUBS, 2, FACE)


def pair_tables(key):
    stream = jax.random.fold_in(key, 23)
    key_present, key_counts, key_sides = jax.random.split(stream, 3)
    present = jax.random.randint(key_present, (SLABS, SUBS, ROUNDS), 0, 4) > 0
    counts = jax.random.randint(key_counts, (SLABS, SUBS, ROUNDS), IFACE // 4, IFACE + 1)
    side_table = jax.random.randint(key_sides, (SLABS, SUBS, ROUNDS, IFACE), 0, 2)
    sub_ids = jnp.arange(SUBS, dtype=jnp.int32)[:, None]
    powers = (2 ** jnp.arange(ROUNDS, dtype=jnp.int32))[None, :]
    partner = jnp.bitwise_xor(sub_ids, powers)
    low_side = jnp.minimum(sub_ids, partner)
    high_side = jnp.maximum(sub_ids, partner)
    round_ids = jnp.broadcast_to(jnp.arange(ROUNDS, dtype=jnp.int32)[None, :], (SUBS, ROUNDS))
    linked = present[:, low_side, round_ids]
    forced_on = ((low_side == 0) | (low_side == SUBS - 2)) & (round_ids == 0)
    forced_off = (low_side == 2) & (round_ids == 0)
    linked = (linked | forced_on[None]) & jnp.logical_not(forced_off)[None]
    filled = (low_side == 0) & (round_ids == 0)
    shared_count = jnp.where(filled[None], IFACE, counts[:, low_side, round_ids])
    shared_count = jnp.where(linked, shared_count, 0)
    partner_ids = jnp.where(linked, partner[None], -1)
    side_bits = side_table[:, low_side, round_ids]
    owner = jnp.where(side_bits == 1, low_side[None, :, :, None], high_side[None, :, :, None])
    slot_ids = jnp.arange(IFACE, dtype=jnp.int32)[None, None, None, :]
    owner = jnp.where(slot_ids < shared_count[..., None], owner, sub_ids[None, :, :, None])
    return (partner_ids.astype(jnp.int32), shared_count.astype(jnp.int32), owner.astype(jnp.int32))


def draw_neighbours(key, part):
    return pair_tables(key)[0]


def draw_iface_count(key, part):
    return pair_tables(key)[1]


def draw_owner_ids(key, part):
    return pair_tables(key)[2]


def steps_of(stream_key, shape, cuts, least, high):
    def one(axis_at, parts):
        steps = jax.random.uniform(jax.random.fold_in(jax.random.fold_in(stream_key, 6), axis_at), (parts,), jnp.float32, least / len(cuts), high / len(cuts))
        return jnp.repeat(jnp.exp(steps), shape[axis_at] // parts).reshape((-1,) + (1,) * (len(shape) - axis_at - 1))

    factor_of = one(*cuts[0])
    for cut in cuts[1:]:
        factor_of = factor_of * one(*cut)
    return factor_of


def gaussian(stream_key, dims, deviation, bound, kind=jnp.bfloat16):
    array = deviation * jax.random.normal(stream_key, dims, jnp.float32)
    return jnp.clip(array, min=-bound, max=bound).astype(kind)


def setup_inputs(seed: int = 0) -> dict:
    key_list = jax.random.split(jax.random.key(seed), 12)
    return {
        "adjoint_load": draw_adjoint_load(jax.random.fold_in(key_list[11], 71), 0),
        "design": jnp.clip(1.0 * jax.random.uniform(key_list[1], (SLABS, SUBS, ELEMS), jnp.float32) ** steps_of(key_list[1], (SLABS, SUBS, ELEMS), ((0, 4), (1, 64)), -0.2, 0.2), 0.0, 1.0),
        "viscous_block": draw_viscous_block(jax.random.fold_in(key_list[11], 71), 0),
        "brinkman_block": draw_brinkman_block(jax.random.fold_in(key_list[11], 71), 0),
        "coupling": gaussian(key_list[4], (8, 24), 0.3, 1.2, jnp.float32),
        "stabilization": draw_stabilization(jax.random.fold_in(key_list[11], 71), 0),
        "neighbours": draw_neighbours(jax.random.fold_in(key_list[11], 71), 0),
        "iface_nodes": draw_iface_nodes(jax.random.fold_in(key_list[11], 71), 0),
        "iface_count": draw_iface_count(jax.random.fold_in(key_list[11], 71), 0),
        "face_nodes": draw_face_nodes(jax.random.fold_in(key_list[11], 71), 0),
        "owner_ids": draw_owner_ids(jax.random.fold_in(key_list[11], 71), 0),
    }


PRECISE = lax.Precision.HIGHEST
BRINKMAN_MAX = 4.0
RAMP_PARAM = 0.1

def corner_offsets(corner):
    return (corner // 4, corner // 2 % 2, corner % 2)

def element_vectors(field):
    channels = field.shape[0]
    node_grid = field.reshape(channels, EX + 1, EY + 1, EZ + 1)
    corner_list = []
    for corner in range(8):
        shift_x, shift_y, shift_z = corner_offsets(corner)
        window = node_grid[:, shift_x:shift_x + EX, shift_y:shift_y + EY, shift_z:shift_z + EZ]
        corner_list.append(window.reshape(channels, ELEMS))
    return jnp.stack(corner_list, axis=1)

def node_sums(element_out):
    channels = element_out.shape[0]
    summed = jnp.zeros((channels, EX + 1, EY + 1, EZ + 1), jnp.float32)
    for corner in range(8):
        shift_x, shift_y, shift_z = corner_offsets(corner)
        corner_block = element_out[:, corner].reshape(channels, EX, EY, EZ)
        summed = summed + jnp.pad(corner_block, ((0, 0), (shift_x, 1 - shift_x), (shift_y, 1 - shift_y), (shift_z, 1 - shift_z)))
    return summed.reshape(channels, NODES)

def brinkman_of(design):
    return BRINKMAN_MAX * RAMP_PARAM * (1.0 - design) / (RAMP_PARAM + design)

def adjoint_terms(state, brinkman, viscous_block, brinkman_block, coupling, stabilization):
    values = element_vectors(state).reshape(CASES, 32, ELEMS)
    velocity = values[:, :24]
    pressure = values[:, 24:]
    out_velocity = jnp.einsum('ij,cie->cje', viscous_block, velocity, precision=PRECISE)
    out_velocity = out_velocity + brinkman * jnp.einsum('ij,cie->cje', brinkman_block, velocity, precision=PRECISE)
    out_velocity = out_velocity + jnp.einsum('kj,cke->cje', coupling, pressure, precision=PRECISE)
    out_pressure = jnp.einsum('kj,cje->cke', coupling, velocity, precision=PRECISE) - jnp.einsum('lk,cle->cke', stabilization, pressure, precision=PRECISE)
    element_out = jnp.concatenate([out_velocity, out_pressure], axis=1).reshape(CASES * 4, 8, ELEMS)
    return node_sums(element_out)

def divergence_terms(velocity_nodes, coupling):
    element_vel = element_vectors(velocity_nodes).reshape(CASES, 24, ELEMS)
    return node_sums(jnp.einsum('kj,cje->cke', coupling, element_vel, precision=PRECISE))

def gradient_terms(pressure_nodes, coupling):
    element_pre = element_vectors(pressure_nodes)
    element_out = jnp.einsum('kj,cke->cje', coupling, element_pre, precision=PRECISE).reshape(CASES * 3, 8, ELEMS)
    return node_sums(element_out)

def diagonal_terms(brinkman, viscous_block, brinkman_block):
    diag_elem = jnp.diagonal(viscous_block)[:, None] + jnp.diagonal(brinkman_block)[:, None] * brinkman[None, :]
    return node_sums(diag_elem.reshape(3, 8, ELEMS))

def schur_terms(diag_nodes, coupling, stabilization):
    inverse = 1.0 / element_vectors(diag_nodes).reshape(24, ELEMS)
    schur_elem = jnp.einsum('kj,je->ke', coupling * coupling, inverse, precision=PRECISE) + jnp.diagonal(stabilization)[:, None]
    return node_sums(schur_elem[None])

def node_weights(iface_nodes, not_owned, lower_face, lower_lost):
    weights = jnp.ones((NODES,), jnp.float32)
    for matching in range(ROUNDS):
        keep = jnp.where(not_owned[matching], 0.0, 1.0).astype(weights.dtype)
        weights = weights.at[iface_nodes[matching]].multiply(keep)
    return weights.at[lower_face].multiply(jnp.where(lower_lost, 0.0, 1.0).astype(weights.dtype))

def add_shared(partial_sums, iface_nodes, incoming, face_nodes, from_below, from_above):
    summed = partial_sums
    for matching in range(ROUNDS):
        summed = summed.at[:, iface_nodes[matching]].add(incoming[matching])
    summed = summed.at[:, face_nodes[0]].add(from_below)
    return summed.at[:, face_nodes[1]].add(from_above)

def assemble(partial_sums, iface_nodes, iface_count, neighbours, face_nodes):
    slot_ids = jnp.arange(IFACE, dtype=jnp.int32)
    slot_valid = (slot_ids < iface_count[..., None]).astype(partial_sums.dtype)
    outgoing = jnp.take_along_axis(partial_sums[:, :, None], iface_nodes[:, :, :, None, :], axis=-1) * slot_valid[:, :, :, None, :]
    partner = jnp.maximum(neighbours, 0).astype(jnp.int32)
    present = (neighbours >= 0).astype(partial_sums.dtype)
    received = []
    for matching in range(ROUNDS):
        chosen = jnp.take_along_axis(outgoing[:, :, matching], partner[:, :, matching, None, None], axis=1)
        received.append(chosen * present[:, :, matching, None, None])
    incoming = jnp.stack(received, axis=2)
    face_out = jnp.take_along_axis(partial_sums[:, :, None], face_nodes[:, :, :, None, :], axis=-1)
    empty_face = jnp.zeros_like(face_out[:1, :, 1])
    from_below = jnp.concatenate([empty_face, face_out[:-1, :, 1]], axis=0)
    from_above = jnp.concatenate([face_out[1:, :, 0], empty_face], axis=0)
    return jax.vmap(jax.vmap(add_shared))(partial_sums, iface_nodes, incoming, face_nodes, from_below, from_above)

def per_device(function, *arrays):
    flattened = tuple((array_item.reshape((SLABS * SUBS,) + array_item.shape[2:]) for array_item in arrays))
    result = lax.map(lambda device_items: function(*device_items), flattened)
    return result.reshape((SLABS, SUBS) + result.shape[1:])

def triangular_solves(factor, target):
    middle = []
    for row_index in range(KRYLOV):
        remainder = target[:, row_index] - sum((factor[:, row_index, col_index] * middle[col_index] for col_index in range(row_index)))
        middle.append(remainder / factor[:, row_index, row_index])
    result = [None] * KRYLOV
    for row_index in reversed(range(KRYLOV)):
        remainder = middle[row_index] - sum((factor[:, col_index, row_index] * result[col_index] for col_index in range(row_index + 1, KRYLOV)))
        result[row_index] = remainder / factor[:, row_index, row_index]
    return jnp.stack(result, axis=1)

def reference(adjoint_load, design, viscous_block, brinkman_block, coupling, stabilization, neighbours, iface_nodes, iface_count, face_nodes, owner_ids):
    brinkman = brinkman_of(design)

    def link(partial_sums):
        return assemble(partial_sums, iface_nodes, iface_count, neighbours, face_nodes)
    slot_ids = jnp.arange(IFACE, dtype=jnp.int32)
    sub_ids = jnp.arange(SUBS, dtype=jnp.int32)[None, :, None, None]
    not_owned = (slot_ids < iface_count[..., None]) & (owner_ids != sub_ids)
    lower_lost = jnp.broadcast_to((jnp.arange(SLABS) > 0)[:, None], (SLABS, SUBS))
    weights = jax.vmap(jax.vmap(node_weights))(iface_nodes, not_owned, face_nodes[:, :, 0], lower_lost)

    def weighted_dot(first_vec, second_vec):
        return lax.optimization_barrier(jnp.sum(weights[:, :, None, None, :] * first_vec * second_vec, axis=(0, 1, 3, 4)))
    owned_load = (adjoint_load * weights[:, :, None, None, :]).reshape(SLABS, SUBS, CASES * 4, NODES)
    diag_part = per_device(partial(diagonal_terms, viscous_block=viscous_block, brinkman_block=brinkman_block), brinkman)
    assembled = link(jnp.concatenate([owned_load, diag_part], axis=2))
    start_vec = assembled[:, :, :CASES * 4].reshape(SLABS, SUBS, CASES, 4, NODES)
    diag_nodes = assembled[:, :, CASES * 4:]
    schur_diag = link(per_device(partial(schur_terms, coupling=coupling, stabilization=stabilization), diag_nodes))[:, :, 0]

    def precondition(vector):
        velocity_guess = vector[:, :, :, :3] / diag_nodes[:, :, None]
        divergence = link(per_device(partial(divergence_terms, coupling=coupling), velocity_guess.reshape(SLABS, SUBS, CASES * 3, NODES)))
        pressure = (divergence - vector[:, :, :, 3]) / schur_diag[:, :, None]
        gradient = link(per_device(partial(gradient_terms, coupling=coupling), pressure)).reshape(SLABS, SUBS, CASES, 3, NODES)
        velocity = velocity_guess - gradient / diag_nodes[:, :, None]
        return jnp.concatenate([velocity, pressure[:, :, :, None]], axis=3)

    def operator(direction):
        image_part = per_device(partial(adjoint_terms, viscous_block=viscous_block, brinkman_block=brinkman_block, coupling=coupling, stabilization=stabilization), direction.reshape(SLABS, SUBS, CASES * 4, NODES), brinkman)
        return link(image_part).reshape(SLABS, SUBS, CASES, 4, NODES)
    start_norm = jnp.sqrt(weighted_dot(start_vec, start_vec))
    krylov_basis = [start_vec / start_norm[None, None, :, None, None]]
    hessenberg = jnp.zeros((CASES, KRYLOV + 1, KRYLOV), jnp.float32)
    directions = []
    for krylov_step in range(KRYLOV):
        direction = precondition(krylov_basis[-1])
        directions.append(direction)
        product_vec = operator(direction)
        heights = jnp.stack([weighted_dot(vector, product_vec) for vector in krylov_basis], axis=1)
        for basis_index in range(len(krylov_basis)):
            product_vec = product_vec - heights[None, None, :, basis_index, None, None] * krylov_basis[basis_index]
        length = jnp.sqrt(weighted_dot(product_vec, product_vec))
        hessenberg = hessenberg.at[:, :krylov_step + 1, krylov_step].set(heights)
        hessenberg = hessenberg.at[:, krylov_step + 1, krylov_step].set(length)
        krylov_basis.append(product_vec / length[None, None, :, None, None])
    normal_matrix = jnp.einsum('cij,cik->cjk', hessenberg, hessenberg, precision=PRECISE)
    target = start_norm[:, None] * hessenberg[:, 0, :]
    factor = jnp.linalg.cholesky(normal_matrix)
    coefficients = triangular_solves(factor, target)
    solution = sum((coefficients[None, None, :, krylov_step, None, None] * directions[krylov_step] for krylov_step in range(KRYLOV)))
    return (solution, coefficients)
```

```python
import jax
import jax.numpy as jnp
from jax import lax
from jax.experimental import pallas as pl
from jax.experimental.pallas import tpu as pltpu
from jax.sharding import PartitionSpec as P

EX = 4
EY = 4
EZ = 127
IFACE = 256
FACE = 512
ROUNDS = 3
KRYLOV = 3
CASES = 2
NODES = 3200
LANES = 128
ROWS = NODES // LANES
ELEM_ROWS = EX * EY
GROUPS = (ROUNDS * IFACE + 2 * FACE) // LANES
SIDE = EY + 1
BRINKMAN_MAX = 4.0
RAMP_PARAM = 0.1
SHIFT = 1.0
PAIRS = [(i, j) for j in range(KRYLOV + 1) for i in range(j + 1)]
SIZES = (IFACE, IFACE, IFACE, FACE, FACE)
F32 = jnp.float32
BF16 = jnp.bfloat16
EXACT = lax.Precision.HIGHEST
VMEM = pl.BlockSpec(memory_space=pltpu.VMEM)
SMEM = pl.BlockSpec(memory_space=pltpu.SMEM)


def iota(shape, dim):
    return lax.broadcasted_iota(jnp.int32, shape, dim)


def dot_nt(left, right, **options):
    return lax.dot_general(
        left, right, (((1,), (1,)), ((), ())), preferred_element_type=F32, **options
    )


def dot_nn(left, right, **options):
    return lax.dot_general(
        left, right, (((1,), (0,)), ((), ())), preferred_element_type=F32, **options
    )


def row_of(ref, r, top=0):
    return ref[top : top + 8, r * LANES : (r + 1) * LANES]


def velocity_rows(shape=(8, LANES)):
    return iota(shape, 0) % 4 != 3


def lane_gather(values, lanes):
    return jnp.take_along_axis(values, lanes, axis=1, mode="promise_in_bounds")


def group_slices():
    for buffer, size in enumerate(SIZES):
        for piece in range(size // LANES):
            yield buffer, slice(piece * LANES, (piece + 1) * LANES)


def gather_slots(field, lane_ref, row_ref, send_refs, tops=(0,)):
    for group, (buffer, at) in enumerate(group_slices()):
        span = slice(group * LANES, (group + 1) * LANES)
        lanes = lane_ref[:, span]
        rows = row_ref[:, span]
        found = [jnp.zeros((8, LANES), F32) for _ in tops]
        for r in range(ROWS):
            here = rows == r
            for k, top in enumerate(tops):
                found[k] = jnp.where(here, lane_gather(row_of(field, r, top), lanes), found[k])
        for k, top in enumerate(tops):
            send_refs[buffer][top : top + 8, at] = found[k]


def scattered(r, hi_ref, lo_ref, recv_refs, top=0):
    hi = row_of(hi_ref, r)
    lo = row_of(lo_ref, r)
    total = jnp.zeros((8, LANES), F32)
    for group, (buffer, at) in enumerate(group_slices()):
        value = lane_gather(recv_refs[buffer][top : top + 8, at], lo)
        total = jnp.where(hi == group + 1, value, total)
    return total


def stage_row(value, r, high_ref, low_ref):
    inside = iota((8, LANES), 1) < EZ
    pair = jnp.concatenate(
        [
            jnp.where(inside, value, 0.0),
            jnp.where(inside, pltpu.roll(value, LANES - 1, 1), 0.0),
        ],
        axis=0,
    )
    high = pair.astype(BF16)
    high_ref[r * 16 : (r + 1) * 16, :] = high
    low_ref[r * 16 : (r + 1) * 16, :] = (pair - high.astype(F32)).astype(BF16)


def element_inputs(high_ref, low_ref, x_ref):
    for e in range(ELEM_ROWS):
        a, b = divmod(e, EY)
        for q in range(4):
            r = (a + q // 2) * SIDE + b + q % 2
            high = high_ref[r * 16 : (r + 1) * 16, :]
            low = low_ref[r * 16 : (r + 1) * 16, :]
            at = slice(e * LANES, (e + 1) * LANES)
            x_ref[q * 16 : (q + 1) * 16, at] = high
            x_ref[64 + q * 16 : 64 + (q + 1) * 16, at] = low
            x_ref[128 + q * 16 : 128 + (q + 1) * 16, at] = high


def corners_at(r):
    i, j = divmod(r, SIDE)
    for q in range(4):
        a, b = i - q // 2, j - q % 2
        if 0 <= a < EX and 0 <= b < EY:
            yield q, a * EY + b


def node_row(r, corner_value):
    parts = [None, None]
    for q, e in corners_at(r):
        for qc in range(2):
            value = corner_value(q, qc, e)
            parts[qc] = value if parts[qc] is None else parts[qc] + value
    return parts[0] + pltpu.roll(parts[1], 1, 1)


def output_corner(o_ref, top=0):
    def corner_value(q, qc, e):
        start = top + (q * 2 + qc) * 8
        return o_ref[start : start + 8, e * LANES : (e + 1) * LANES]

    return corner_value


def own_ids(rows, cols, dim):
    at = iota((rows, cols), dim) % 64
    return at // 8, at % 4


def select_velocity(rows):
    corner, field = own_ids(rows, 24, 0)
    entry = iota((rows, 24), 1)
    return ((entry // 8 == field) & (entry % 8 == corner)).astype(F32)


def select_field(rows, wanted):
    corner, field = own_ids(rows, 8, 0)
    entry = iota((rows, 8), 1)
    return ((field == wanted) & (entry == corner)).astype(F32)


def setup_kernel(
    count_ref,
    neighbour_ref,
    load_ref,
    design_ref,
    viscous_ref,
    brink_ref,
    iface_ref,
    face_ref,
    owner_ref,
    own_ref,
    lane_ref,
    row_ref,
    hi_ref,
    lo_ref,
    weight_ref,
    brinkman_ref,
    *send_refs,
):
    sub = lax.axis_index("sub")
    slab = lax.axis_index("slab")
    slabs = lax.axis_size("slab")
    even = slab % 2 == 0
    lanes = iota((1, LANES), 1)
    node_list, used_list, lost_list = [], [], []
    for matching in range(ROUNDS):
        limit = jnp.where(neighbour_ref[0, 0, matching] >= 0, count_ref[0, 0, matching], 0)
        for piece in range(IFACE // LANES):
            span = slice(piece * LANES, (piece + 1) * LANES)
            used = lanes + piece * LANES < limit
            node_list.append(iface_ref[0, 0, matching : matching + 1, span])
            used_list.append(used.astype(jnp.int32))
            counted = lanes + piece * LANES < count_ref[0, 0, matching]
            away = owner_ref[0, 0, matching : matching + 1, span] != sub
            lost_list.append((counted & away).astype(jnp.int32))
    for swap in range(2):
        upper = even if swap == 0 else jnp.logical_not(even)
        there = jnp.where(upper, slab < slabs - 1, slab > 0)
        gone = jnp.logical_and(jnp.logical_not(upper), slab > 0)
        for piece in range(FACE // LANES):
            span = slice(piece * LANES, (piece + 1) * LANES)
            node_list.append(
                jnp.where(upper, face_ref[0, 0, 1:2, span], face_ref[0, 0, 0:1, span])
            )
            used_list.append(jnp.full((1, LANES), there.astype(jnp.int32)))
            lost_list.append(jnp.full((1, LANES), gone.astype(jnp.int32)))
    slots = GROUPS * LANES
    nodes = jnp.concatenate(node_list, axis=1)
    used = jnp.concatenate(used_list, axis=1)
    lost = jnp.concatenate(lost_list, axis=1)
    node_lane = nodes % LANES
    node_rows = nodes // LANES
    lane_ref[...] = jnp.broadcast_to(node_lane, (8, slots))
    row_ref[...] = jnp.broadcast_to(node_rows, (8, slots))
    slot = iota((1, slots), 1)
    match = iota((32, slots), 0) == node_rows
    codes = jnp.concatenate(
        [
            jnp.where(match, (used * (slot // LANES + 1)).astype(F32), 0.0),
            jnp.where(match, (used * (slot % LANES)).astype(F32), 0.0),
            jnp.where(match, lost.astype(F32), 0.0),
        ],
        axis=0,
    ).astype(BF16)
    spread = (iota((LANES, slots), 0) == node_lane).astype(F32).astype(BF16)
    tables = dot_nt(codes, spread)

    dark = RAMP_PARAM + design_ref[...]
    flat = BRINKMAN_MAX * RAMP_PARAM * (1.0 - design_ref[...]) / dark
    column = iota((1, LANES), 1)
    inside = column < EZ
    for e in range(ELEM_ROWS):
        line = pltpu.roll(jnp.broadcast_to(flat[e : e + 1, :], (8, LANES)), e, 1)[0:1]
        if e > 0:
            before = pltpu.roll(jnp.broadcast_to(flat[e - 1 : e, :], (8, LANES)), e, 1)[0:1]
            line = jnp.where(column < e, before, line)
        brinkman_ref[e : e + 1, :] = jnp.where(inside, line, 0.0)

    eye = (iota((24, 24), 0) == iota((24, 24), 1)).astype(F32)
    pick = select_velocity(64)
    viscous_diag = jnp.sum(
        dot_nt(pick, viscous_ref[...] * eye, precision=EXACT), axis=1, keepdims=True
    )
    brink_diag = jnp.sum(dot_nt(pick, brink_ref[...] * eye, precision=EXACT), axis=1, keepdims=True)

    def diagonal(q, qc, e):
        start = (q * 2 + qc) * 8
        value = (
            viscous_diag[start : start + 8] + brink_diag[start : start + 8] * brinkman_ref[e : e + 1, :]
        )
        return jnp.where(inside, value, 0.0)

    for r in range(ROWS):
        at = slice(r * LANES, (r + 1) * LANES)
        hi_ref[:, at] = jnp.broadcast_to(tables[r : r + 1].astype(jnp.int32), (8, LANES))
        lo_ref[:, at] = jnp.broadcast_to(tables[32 + r : 33 + r].astype(jnp.int32), (8, LANES))
        weight = 1.0 - jnp.broadcast_to(tables[64 + r : 65 + r], (8, LANES))
        weight_ref[:, at] = weight
        load = jnp.concatenate([load_ref[0, 0, 0, :, at], load_ref[0, 0, 1, :, at]], axis=0)
        own_ref[0:8, at] = load * weight
        own_ref[8:16, at] = node_row(r, diagonal)
    gather_slots(own_ref, lane_ref, row_ref, send_refs, (0, 8))


def matrix_kernel(
    viscous_ref,
    brink_ref,
    coupling_ref,
    stab_ref,
    divergence_ref,
    schur_ref,
    gradient_ref,
    image_ref,
    bias_ref,
):
    velocity, velocity_in = select_velocity(64), select_velocity(192)
    pressure, pressure_in = select_field(64, 3), select_field(192, 3)
    coupling = coupling_ref[...]
    same = (iota((64, 192), 0) // 4) % 2 == (iota((64, 192), 1) // 4) % 2
    coarse = iota((64, 192), 1) < 128

    def parts(whole):
        whole = jnp.where(same, whole, 0.0)
        high = whole.astype(BF16).astype(F32)
        return jnp.where(coarse, high, whole - high).astype(BF16)

    def nn(left, right):
        return dot_nn(left, right, precision=EXACT)

    def nt(left, right):
        return dot_nt(left, right, precision=EXACT)

    down = nt(nn(pressure, coupling), velocity_in)
    up = nt(nt(velocity, coupling), pressure_in)
    divergence_ref[...] = parts(down)
    gradient_ref[...] = parts(up)
    schur_ref[...] = parts(nt(nn(select_field(64, 0), coupling * coupling), velocity_in))
    from_velocity = iota((64, 192), 1) % 4 != 3
    to_velocity = iota((64, 192), 0) % 4 != 3
    viscous = nt(nt(velocity, viscous_ref[...]), velocity_in)
    stab = nt(nt(pressure, stab_ref[...]), pressure_in)
    image_ref[0:64, :] = parts(
        jnp.where(
            to_velocity,
            jnp.where(from_velocity, viscous, up),
            jnp.where(from_velocity, down, -stab),
        )
    )
    image_ref[64:128, :] = parts(nt(nt(velocity, brink_ref[...]), velocity_in))
    eye = (iota((8, 8), 0) == iota((8, 8), 1)).astype(F32)
    bias = jnp.sum(nt(select_field(64, 0), stab_ref[...] * eye), axis=1, keepdims=True)
    bias_ref[...] = jnp.where(iota((64, LANES), 1) < EZ, bias, 0.0)


def diagonal_kernel(
    own_ref,
    lane_ref,
    row_ref,
    hi_ref,
    lo_ref,
    divergence_ref,
    schur_ref,
    bias_ref,
    *refs,
):
    recv_refs, (vector_ref, inverse_ref, part_ref) = refs[:5], refs[5:8]
    send_refs = refs[8:13]
    high_ref, low_ref, x_ref, o_ref = refs[13:]
    for r in range(ROWS):
        at = slice(r * LANES, (r + 1) * LANES)
        vector_ref[:, at] = row_of(own_ref, r) + scattered(r, hi_ref, lo_ref, recv_refs)
        diag = row_of(own_ref, r, 8) + scattered(r, hi_ref, lo_ref, recv_refs, 8)
        inverse = jnp.where(velocity_rows(), 1.0 / diag, 0.0)
        inverse_ref[:, at] = inverse
        stage_row(inverse, r, high_ref, low_ref)
    element_inputs(high_ref, low_ref, x_ref)
    o_ref[...] = dot_nn(schur_ref[...], x_ref[...])
    for r in range(ROWS):
        stage_row(row_of(vector_ref, r) * row_of(inverse_ref, r), r, high_ref, low_ref)
    element_inputs(high_ref, low_ref, x_ref)
    o_ref[...] += dot_nn(divergence_ref[...], x_ref[...])
    output = output_corner(o_ref)

    def with_bias(q, qc, e):
        start = (q * 2 + qc) * 8
        return output(q, qc, e) + bias_ref[start : start + 8, :]

    for r in range(ROWS):
        part_ref[:, r * LANES : (r + 1) * LANES] = node_row(r, with_bias)
    gather_slots(part_ref, lane_ref, row_ref, send_refs)


def divergence_kernel(
    part_ref, inverse_ref, lane_ref, row_ref, hi_ref, lo_ref, divergence_ref, *refs
):
    recv_refs, (vector_ref, out_ref) = refs[:5], refs[5:7]
    send_refs = refs[7:12]
    high_ref, low_ref, x_ref, o_ref = refs[12:]
    for r in range(ROWS):
        at = slice(r * LANES, (r + 1) * LANES)
        vector = row_of(part_ref, r) + scattered(r, hi_ref, lo_ref, recv_refs)
        vector_ref[:, at] = vector
        stage_row(vector * row_of(inverse_ref, r), r, high_ref, low_ref)
    element_inputs(high_ref, low_ref, x_ref)
    o_ref[...] = dot_nn(divergence_ref[...], x_ref[...])
    output = output_corner(o_ref)
    for r in range(ROWS):
        out_ref[:, r * LANES : (r + 1) * LANES] = node_row(r, output)
    gather_slots(out_ref, lane_ref, row_ref, send_refs)


def gradient_kernel(first, *refs):
    part_ref, vector_ref = refs[:2]
    refs = refs[2:]
    if not first:
        schur_ref, refs = refs[0], refs[1:]
    lane_ref, row_ref, hi_ref, lo_ref, gradient_ref = refs[:5]
    recv_refs, refs = refs[5:10], refs[10:]
    if first:
        schur_ref, refs = refs[0], refs[1:]
    pressure_ref, out_ref = refs[:2]
    send_refs = refs[2:7]
    high_ref, low_ref, x_ref, o_ref = refs[7:]
    for r in range(ROWS):
        at = slice(r * LANES, (r + 1) * LANES)
        summed = row_of(part_ref, r) + scattered(r, hi_ref, lo_ref, recv_refs)
        if first:
            schur = pltpu.roll(summed, 3, 0)
            schur_ref[:, at] = jnp.where(velocity_rows(), 0.0, 1.0 / schur)
        pressure = (summed - row_of(vector_ref, r)) * row_of(schur_ref, r)
        pressure_ref[:, at] = pressure
        stage_row(pressure, r, high_ref, low_ref)
    element_inputs(high_ref, low_ref, x_ref)
    o_ref[...] = dot_nn(gradient_ref[...], x_ref[...])
    output = output_corner(o_ref)
    for r in range(ROWS):
        out_ref[:, r * LANES : (r + 1) * LANES] = node_row(r, output)
    gather_slots(out_ref, lane_ref, row_ref, send_refs)


def image_kernel(
    part_ref,
    vector_ref,
    pressure_ref,
    inverse_ref,
    brinkman_ref,
    lane_ref,
    row_ref,
    hi_ref,
    lo_ref,
    image_ref,
    *refs,
):
    recv_refs, (direction_ref, out_ref) = refs[:5], refs[5:7]
    send_refs = refs[7:12]
    high_ref, low_ref, x_ref, o_ref = refs[12:]
    for r in range(ROWS):
        at = slice(r * LANES, (r + 1) * LANES)
        gradient = row_of(part_ref, r) + scattered(r, hi_ref, lo_ref, recv_refs)
        direction = (row_of(vector_ref, r) - gradient) * row_of(inverse_ref, r) + row_of(
            pressure_ref, r
        )
        direction_ref[:, at] = direction
        stage_row(direction, r, high_ref, low_ref)
    element_inputs(high_ref, low_ref, x_ref)
    o_ref[...] = dot_nn(image_ref[...], x_ref[...])
    viscous, brink = output_corner(o_ref), output_corner(o_ref, 64)

    def corner_value(q, qc, e):
        return viscous(q, qc, e) + brink(q, qc, e) * brinkman_ref[e : e + 1, :]

    for r in range(ROWS):
        share = jnp.where(row_of(hi_ref, r) > 0, 0.5 * SHIFT, SHIFT)
        out_ref[:, r * LANES : (r + 1) * LANES] = (
            node_row(r, corner_value) - share * row_of(vector_ref, r)
        )
    gather_slots(out_ref, lane_ref, row_ref, send_refs)


def largest(ref):
    top = jnp.abs(row_of(ref, 0))
    for r in range(1, ROWS):
        top = jnp.maximum(top, jnp.abs(row_of(ref, r)))
    top = jnp.max(top, axis=1, keepdims=True)
    return jnp.where(top > 0.0, top, 1.0)


def gram_kernel(newest, *refs):
    vectors, (weight_ref, old_ref), out_ref = refs[: newest + 1], refs[newest + 1 : -1], refs[-1]
    if newest == 1:
        fresh = (0, 1)
    else:
        fresh = (newest,)
    scales = {}
    for i in range(newest + 1):
        if i in fresh:
            scales[i] = largest(vectors[i])
        else:
            scales[i] = old_ref[8 * (1 + i) : 8 * (2 + i), 0:1]
    inverse = {i: 1.0 / scales[i] for i in scales}
    pairs = [(i, j) for i, j in PAIRS if j in fresh]
    totals = {pair: jnp.zeros((8, LANES), F32) for pair in pairs}
    last = newest == KRYLOV
    for r in range(ROWS):
        rows = {i: row_of(vectors[i], r) * inverse[i] for i in range(newest + 1)}
        if last:
            weight = jnp.where(row_of(weight_ref, r) > 0, 0.0, 1.0)
        else:
            weight = row_of(weight_ref, r)
        for i, j in pairs:
            product = rows[i] * rows[j]
            if not last or i == j:
                product = product * weight
            totals[i, j] = totals[i, j] + product
    lane = iota((8, LANES), 1)
    if newest == 1:
        dots = jnp.zeros((8, LANES), F32)
    else:
        dots = old_ref[0:8, :]
    for i, j in pairs:
        at = PAIRS.index((i, j))
        dots = jnp.where(lane == at, jnp.sum(totals[i, j], axis=1, keepdims=True), dots)
    out_ref[0:8, :] = dots
    for i in range(KRYLOV + 1):
        at = slice(8 * (1 + i), 8 * (2 + i))
        if i in scales:
            out_ref[at, :] = jnp.broadcast_to(scales[i], (8, LANES))
        elif newest == 1:
            out_ref[at, :] = jnp.ones((8, LANES), F32)
        else:
            out_ref[at, :] = old_ref[at, :]


def norm_kernel(gram_ref, lane_ref, count_ref, neighbour_ref, *refs):
    send_refs, recv_refs, out_ref = refs[:5], refs[5:10], refs[10]
    slab = lax.axis_index("slab")
    slabs = lax.axis_size("slab")
    even = slab % 2 == 0
    inverse = 1.0 / gram_ref[8 * (1 + KRYLOV) : 8 * (2 + KRYLOV), 0:1]
    lane = iota((8, LANES), 1)
    total = jnp.zeros((8, LANES), F32)
    for buffer, at in group_slices():
        if buffer < ROUNDS:
            limit = jnp.where(neighbour_ref[0, 0, buffer] >= 0, count_ref[0, 0, buffer], 0)
            used = lane + at.start < limit
        else:
            upper = even if buffer == ROUNDS else jnp.logical_not(even)
            there = jnp.where(upper, slab < slabs - 1, slab > 0)
            used = jnp.full((8, LANES), there.astype(jnp.int32)) > 0
        value = (send_refs[buffer][:, at] + recv_refs[buffer][:, at]) * inverse
        total = total + jnp.where(used, value * value, 0.0)
    both = 0.5 * jnp.sum(total, axis=1, keepdims=True)
    at = PAIRS.index((KRYLOV, KRYLOV))
    out_ref[0:8, :] = gram_ref[0:8, :] + jnp.where(lane == at, both, 0.0)
    for side in range(2):
        scale = jnp.ones((8, LANES), F32)
        for entry, pair in enumerate(PAIRS):
            k = pair[side]
            scale = jnp.where(lane == entry, gram_ref[8 * (1 + k) : 8 * (2 + k), :], scale)
        out_ref[8 * (1 + side) : 8 * (2 + side), :] = scale


def merged(items):
    tops = []
    for side in (1, 2):
        top = items[0][side]
        for item in items[1:]:
            top = jnp.maximum(top, item[side])
        tops.append(top)
    inverse = [1.0 / top for top in tops]
    total = None
    for dots, left, right in items:
        value = dots * (left * inverse[0]) * (right * inverse[1])
        total = value if total is None else total + value
    return total, tops[0], tops[1]


def planes(ref):
    return ref[0:8, :], ref[8:16, :], ref[16:24, :]


def merge_kernel(*refs):
    for k, value in enumerate(merged([planes(ref) for ref in refs[:-1]])):
        refs[-1][8 * k : 8 * (k + 1), :] = value


def solve_kernel(*refs):
    gram_refs, direction_refs = refs[:4], refs[4:7]
    solution_ref, coefficient_ref = refs[7:]
    whole = merged([planes(ref) for ref in gram_refs])
    cases = []
    for case in range(CASES):
        channels = [
            tuple(plane[4 * case + f : 4 * case + f + 1, :] for plane in whole) for f in range(4)
        ]
        cases.append(merged(channels))
    dots, left, right = [jnp.concatenate([item[k] for item in cases], axis=0) for k in range(3)]
    lane = iota((CASES, LANES), 1)

    def entry(values, pair):
        at = PAIRS.index(pair)
        return jnp.sum(jnp.where(lane == at, values, 0.0), axis=1, keepdims=True)

    size = KRYLOV + 1
    scale = [entry(right, (j, j)) for j in range(size)]
    upper = {}
    for j in range(size):
        for i in range(j + 1):
            value = entry(dots, (i, j))
            for k in range(i):
                value = value - upper[k, i] * upper[k, j]
            upper[i, j] = jnp.sqrt(value) if i == j else value / upper[i, i]
    step = [scale[j + 1] / scale[j] for j in range(KRYLOV)]
    h = {}
    for i in range(size):
        line = []
        for j in range(KRYLOV):
            value = jnp.zeros_like(scale[0])
            if i <= j:
                value = value + SHIFT * upper[i, j]
            if i <= j + 1:
                value = value + upper[i, j + 1] * step[j]
            line.append(value)
        for j in range(KRYLOV):
            value = line[j]
            for k in range(j):
                value = value - h[i, k] * upper[k, j]
            h[i, j] = value / upper[j, j] if i <= j + 1 else jnp.zeros_like(scale[0])
    beta = scale[0] * upper[0, 0]
    target = [beta * h[0, j] for j in range(KRYLOV)]
    factor = {}
    for j in range(KRYLOV):
        for i in range(j, KRYLOV):
            value = sum(h[m, i] * h[m, j] for m in range(size))
            for k in range(j):
                value = value - factor[i, k] * factor[j, k]
            factor[i, j] = jnp.sqrt(value) if i == j else value / factor[j, j]
    middle = []
    for i in range(KRYLOV):
        rest = target[i]
        for k in range(i):
            rest = rest - factor[i, k] * middle[k]
        middle.append(rest / factor[i, i])
    y = [None] * KRYLOV
    for i in reversed(range(KRYLOV)):
        rest = middle[i]
        for k in range(i + 1, KRYLOV):
            rest = rest - factor[k, i] * y[k]
        y[i] = rest / factor[i, i]
    for i in range(KRYLOV):
        coefficient_ref[:, i : i + 1] = y[i]
    c = [None] * KRYLOV
    for i in reversed(range(KRYLOV)):
        rest = y[i]
        for k in range(i + 1, KRYLOV):
            rest = rest - upper[i, k] * c[k]
        c[i] = rest / upper[i, i]
    c = [c[i] / scale[i] for i in range(KRYLOV)]
    for case in range(CASES):
        factors = [jnp.broadcast_to(c[i][case : case + 1], (4, LANES)) for i in range(KRYLOV)]
        for r in range(ROWS):
            at = slice(r * LANES, (r + 1) * LANES)
            span = slice(4 * case, 4 * case + 4)
            value = factors[0] * direction_refs[0][span, at]
            for i in range(1, KRYLOV):
                value = value + factors[i] * direction_refs[i][span, at]
            solution_ref[0, 0, case, :, at] = value


def field(rows=8, cols=NODES, kind=F32):
    return jax.ShapeDtypeStruct((rows, cols), kind)


def sends(rows=8):
    return [field(rows, size) for size in SIZES]


STENCIL = [
    pltpu.VMEM((ROWS * 16, LANES), BF16),
    pltpu.VMEM((ROWS * 16, LANES), BF16),
    pltpu.VMEM((192, ELEM_ROWS * LANES), BF16),
]


def stencil(rows=64):
    return STENCIL + [pltpu.VMEM((rows, ELEM_ROWS * LANES), F32)]


def call(kernel, outs, args, name, smem=(), scratch=(), cost=2000):
    return pl.pallas_call(
        kernel,
        out_shape=outs,
        in_specs=[SMEM if i in smem else VMEM for i in range(len(args))],
        out_specs=jax.tree.map(lambda _: VMEM, outs),
        scratch_shapes=scratch,
        name=name,
        compiler_params=pltpu.CompilerParams(vmem_limit_bytes=8 << 20),
        cost_estimate=pl.CostEstimate(flops=cost * 1000, bytes_accessed=cost * 1000, transcendentals=0),
    )(*args)


def exclusive(count, masks):
    return [[(i, i ^ mask) for i in range(count)] for mask in masks]


def exchange(buffers):
    subs = exclusive(lax.axis_size("sub"), (1, 2, 4))
    slabs = lax.axis_size("slab")
    first = [(i, i ^ 1) for i in range(slabs)]
    second = [(i, ((i + 1) ^ 1) - 1 if 0 < i < slabs - 1 else slabs - 1 - i) for i in range(slabs)]
    routes = [("sub", route) for route in subs] + [("slab", first), ("slab", second)]
    received = [None] * len(buffers)
    for k in (2, 3, 4, 1, 0):
        received[k] = lax.ppermute(buffers[k], *routes[k])
    return received


def spread(item, axis, masks):
    return [lax.ppermute(item, axis, route) for route in exclusive(lax.axis_size(axis), masks)]


def per_device(
    adjoint_load,
    design,
    viscous_block,
    brinkman_block,
    coupling,
    stabilization,
    neighbours,
    iface_nodes,
    iface_count,
    face_nodes,
    owner_ids,
):
    slots = GROUPS * LANES
    flat_design = jnp.pad(design[0, 0], (0, ELEM_ROWS)).reshape(ELEM_ROWS, LANES)
    outs = call(
        setup_kernel,
        [
            field(16),
            field(8, slots, jnp.int32),
            field(8, slots, jnp.int32),
            field(kind=jnp.int32),
            field(kind=jnp.int32),
            field(),
            field(ELEM_ROWS, LANES),
        ]
        + sends(16),
        (
            iface_count,
            neighbours,
            adjoint_load,
            flat_design,
            viscous_block,
            brinkman_block,
            iface_nodes,
            face_nodes,
            owner_ids,
        ),
        "setup",
        smem=(0, 1),
    )
    own, lanes, rows, hi, lo, weights, brinkman = outs[:7]
    received = exchange(outs[7:])
    divergence_map, schur_map, gradient_map, image_map, bias = call(
        matrix_kernel,
        [field(64, 192, BF16)] * 3 + [field(128, 192, BF16), field(64, LANES)],
        (viscous_block, brinkman_block, coupling, stabilization),
        "matrices",
    )
    tables = (lanes, rows, hi, lo)
    outs = call(
        diagonal_kernel,
        [field(), field(), field()] + sends(),
        (own, *tables, divergence_map, schur_map, bias, *received),
        "diagonal",
        scratch=stencil(),
    )
    vector, inverse, part = outs[:3]
    basis, directions = [vector], []
    schur = None
    gram = None
    for step in range(KRYLOV):
        received = exchange(outs[-5:])
        if step == 0:
            schur, pressure, part, *outs = call(
                lambda *refs: gradient_kernel(True, *refs),
                [field(), field(), field()] + sends(),
                (part, vector, *tables, gradient_map, *received),
                "gradient_first",
                scratch=stencil(),
            )
        else:
            gram = call(
                lambda *refs, newest=step: gram_kernel(newest, *refs),
                field(40, LANES),
                (*basis, weights, weights if gram is None else gram),
                f"gram{step}",
                cost=500,
            )
            pressure, part, *outs = call(
                lambda *refs: gradient_kernel(False, *refs),
                [field(), field()] + sends(),
                (part, vector, schur, *tables, gradient_map, *received),
                "gradient",
                scratch=stencil(),
            )
        received = exchange(outs)
        direction, part, *outs = call(
            image_kernel,
            [field(), field()] + sends(),
            (part, vector, pressure, inverse, brinkman, *tables, image_map, *received),
            "image",
            scratch=stencil(128),
        )
        directions.append(direction)
        received = exchange(outs)
        if step < KRYLOV - 1:
            vector, part, *outs = call(
                divergence_kernel,
                [field(), field()] + sends(),
                (part, inverse, *tables, divergence_map, *received),
                "divergence",
                scratch=stencil(),
            )
            basis.append(vector)
    gram = call(
        lambda *refs: gram_kernel(KRYLOV, *refs),
        field(40, LANES),
        (*basis, part, hi, gram),
        "gram_last",
        cost=500,
    )
    item = call(
        norm_kernel,
        field(24, LANES),
        (gram, lanes, iface_count, neighbours, *outs, *received),
        "norm",
        smem=(2, 3),
    )
    for axis, masks in (("sub", (1, 2, 3)), ("sub", (4, 8, 12)), ("sub", (16, 32, 48))):
        item = call(
            merge_kernel, field(24, LANES), (item, *spread(item, axis, masks)), "merge", cost=10
        )
    return tuple(
        call(
            solve_kernel,
            [
                jax.ShapeDtypeStruct((1, 1, CASES, 4, NODES), F32),
                jax.ShapeDtypeStruct((CASES, KRYLOV), F32),
            ],
            (item, *spread(item, "slab", (1, 2, 3)), *directions),
            "solve",
        )
    )


def solution(mesh):
    placed = (
        P("slab", "sub", None, None, None),
        P("slab", "sub", None),
        P(),
        P(),
        P(),
        P(),
        P("slab", "sub", None),
        P("slab", "sub", None, None),
        P("slab", "sub", None),
        P("slab", "sub", None, None),
        P("slab", "sub", None, None),
    )
    return jax.shard_map(
        per_device,
        mesh=mesh,
        in_specs=placed,
        out_specs=(P("slab", "sub", None, None, None), P()),
        check_vma=False,
    )
```

```python
import jax
import jax.numpy as jnp
from jax import lax
from jax.experimental import pallas as pl
from jax.experimental.pallas import tpu as pltpu
from jax.sharding import PartitionSpec as P

EX = 4
EY = 4
EZ = 127
IFACE = 256
FACE = 512
ROUNDS = 3
KRYLOV = 3
CASES = 2
NODES = 3200
LANES = 128
ROWS = NODES // LANES
ELEM_ROWS = EX * EY
GROUPS = (ROUNDS * IFACE + 2 * FACE) // LANES
SIDE = EY + 1
BRINKMAN_MAX = 4.0
RAMP_PARAM = 0.1
SHIFT = 1.0
PAIRS = [(i, j) for j in range(KRYLOV + 1) for i in range(j + 1)]
SIZES = (IFACE, IFACE, IFACE, FACE, FACE)
F32 = jnp.float32
BF16 = jnp.bfloat16
EXACT = lax.Precision.HIGHEST
VMEM = pl.BlockSpec(memory_space=pltpu.VMEM)
SMEM = pl.BlockSpec(memory_space=pltpu.SMEM)


def iota(shape, dim):
    return lax.broadcasted_iota(jnp.int32, shape, dim)


def dot_nt(left, right, **options):
    return lax.dot_general(
        left, right, (((1,), (1,)), ((), ())), preferred_element_type=F32, **options
    )


def dot_nn(left, right, **options):
    return lax.dot_general(
        left, right, (((1,), (0,)), ((), ())), preferred_element_type=F32, **options
    )


def row_of(ref, r, top=0):
    return ref[top : top + 8, r * LANES : (r + 1) * LANES]


def velocity_rows(shape=(8, LANES)):
    return iota(shape, 0) % 4 != 3


def lane_gather(values, lanes):
    return jnp.take_along_axis(values, lanes, axis=1, mode="promise_in_bounds")


def group_slices():
    for buffer, size in enumerate(SIZES):
        for piece in range(size // LANES):
            yield buffer, slice(piece * LANES, (piece + 1) * LANES)


def gather_slots(fields, lane_ref, row_ref, send_refs):
    for group, (buffer, at) in enumerate(group_slices()):
        span = slice(group * LANES, (group + 1) * LANES)
        lanes = lane_ref[:, span]
        rows = row_ref[:, span]
        found = [jnp.zeros((8, LANES), F32) for _ in fields]
        for r in range(ROWS):
            here = rows == r
            for k, values in enumerate(fields):
                found[k] = jnp.where(here, lane_gather(values[r], lanes), found[k])
        for k, value in enumerate(found):
            send_refs[buffer][8 * k : 8 * k + 8, at] = value


def scattered(own, hi_ref, lo_ref, recv_refs, top=0):
    summed = []
    pieces = [recv_refs[buffer][top : top + 8, at] for buffer, at in group_slices()]
    for r in range(ROWS):
        hi = row_of(hi_ref, r)
        lo = row_of(lo_ref, r)
        total = jnp.zeros((8, LANES), F32)
        for group, piece in enumerate(pieces):
            total = jnp.where(hi == group + 1, lane_gather(piece, lo), total)
        summed.append(own[r] + total)
    return summed


def rows_of(ref, top=0):
    return [row_of(ref, r, top) for r in range(ROWS)]


def put_rows(ref, values, top=0):
    for r, value in enumerate(values):
        ref[top : top + 8, r * LANES : (r + 1) * LANES] = value


def stage(values, x_ref):
    inside = iota((8, LANES), 1) < EZ
    shifted = [pltpu.roll(value, LANES - 1, 1) for value in values]
    for r in range(ROWS):
        pair = jnp.concatenate(
            [jnp.where(inside, values[r], 0.0), jnp.where(inside, shifted[r], 0.0)], axis=0
        )
        high = pair.astype(BF16)
        low = (pair - high.astype(F32)).astype(BF16)
        for q, e in corners_at(r):
            at = slice(e * LANES, (e + 1) * LANES)
            x_ref[q * 16 : (q + 1) * 16, at] = high
            x_ref[64 + q * 16 : 64 + (q + 1) * 16, at] = low
            x_ref[128 + q * 16 : 128 + (q + 1) * 16, at] = high


def corners_at(r):
    i, j = divmod(r, SIDE)
    for q in range(4):
        a, b = i - q // 2, j - q % 2
        if 0 <= a < EX and 0 <= b < EY:
            yield q, a * EY + b


def node_row(r, corner_value):
    parts = [None, None]
    for q, e in corners_at(r):
        for qc in range(2):
            value = corner_value(q, qc, e)
            parts[qc] = value if parts[qc] is None else parts[qc] + value
    return parts[0] + pltpu.roll(parts[1], 1, 1)


def output_corner(o_ref, top=0):
    def corner_value(q, qc, e):
        start = top + (q * 2 + qc) * 8
        return o_ref[start : start + 8, e * LANES : (e + 1) * LANES]

    return corner_value


def own_ids(rows, cols, dim):
    at = iota((rows, cols), dim) % 64
    return at // 8, at % 4


def select_velocity(rows):
    corner, field = own_ids(rows, 24, 0)
    entry = iota((rows, 24), 1)
    return ((entry // 8 == field) & (entry % 8 == corner)).astype(F32)


def select_field(rows, wanted):
    corner, field = own_ids(rows, 8, 0)
    entry = iota((rows, 8), 1)
    return ((field == wanted) & (entry == corner)).astype(F32)


def setup_kernel(
    count_ref,
    neighbour_ref,
    load_ref,
    design_ref,
    viscous_ref,
    brink_ref,
    iface_ref,
    face_ref,
    owner_ref,
    own_ref,
    lane_ref,
    row_ref,
    hi_ref,
    lo_ref,
    weight_ref,
    brinkman_ref,
    *send_refs,
):
    sub = lax.axis_index("sub")
    slab = lax.axis_index("slab")
    slabs = lax.axis_size("slab")
    even = slab % 2 == 0
    lanes = iota((1, LANES), 1)
    node_list, used_list, lost_list = [], [], []
    for matching in range(ROUNDS):
        limit = jnp.where(neighbour_ref[0, 0, matching] >= 0, count_ref[0, 0, matching], 0)
        for piece in range(IFACE // LANES):
            used = lanes + piece * LANES < limit
            line = matching * (IFACE // LANES) + piece
            node_list.append(iface_ref[line : line + 1, :])
            used_list.append(used.astype(jnp.int32))
            counted = lanes + piece * LANES < count_ref[0, 0, matching]
            away = owner_ref[line : line + 1, :] != sub
            lost_list.append((counted & away).astype(jnp.int32))
    for swap in range(2):
        upper = even if swap == 0 else jnp.logical_not(even)
        there = jnp.where(upper, slab < slabs - 1, slab > 0)
        gone = jnp.logical_and(jnp.logical_not(upper), slab > 0)
        for piece in range(FACE // LANES):
            low, high = piece, FACE // LANES + piece
            node_list.append(
                jnp.where(upper, face_ref[high : high + 1, :], face_ref[low : low + 1, :])
            )
            used_list.append(jnp.full((1, LANES), there.astype(jnp.int32)))
            lost_list.append(jnp.full((1, LANES), gone.astype(jnp.int32)))
    slots = GROUPS * LANES
    nodes = jnp.concatenate(node_list, axis=1)
    used = jnp.concatenate(used_list, axis=1)
    lost = jnp.concatenate(lost_list, axis=1)
    node_lane = nodes % LANES
    node_rows = nodes // LANES
    lane_ref[...] = jnp.broadcast_to(node_lane, (8, slots))
    row_ref[...] = jnp.broadcast_to(node_rows, (8, slots))
    slot = iota((1, slots), 1)
    match = iota((32, slots), 0) == node_rows
    codes = jnp.concatenate(
        [
            jnp.where(match, (used * (slot // LANES + 1)).astype(F32), 0.0),
            jnp.where(match, (used * (slot % LANES)).astype(F32), 0.0),
            jnp.where(match, lost.astype(F32), 0.0),
        ],
        axis=0,
    ).astype(BF16)
    spread = (iota((LANES, slots), 0) == node_lane).astype(F32).astype(BF16)
    tables = dot_nt(codes, spread)

    column = iota((1, LANES), 1)
    inside = column < EZ
    line = None
    for e in range(ELEM_ROWS):
        before = line
        at = slice(e * LANES, min((e + 1) * LANES, ELEM_ROWS * EZ))
        design = design_ref[:, at]
        line = BRINKMAN_MAX * RAMP_PARAM * (1.0 - design) / (RAMP_PARAM + design)
        if line.shape[1] < LANES:
            line = jnp.concatenate([line, jnp.zeros((1, LANES - line.shape[1]), F32)], axis=1)
        line = jnp.broadcast_to(line, (8, LANES))
        whole = pltpu.roll(line, e, 1)[0:1]
        if e > 0:
            whole = jnp.where(column < e, pltpu.roll(before, e, 1)[0:1], whole)
        brinkman_ref[e : e + 1, :] = jnp.where(inside, whole, 0.0)

    eye = (iota((24, 24), 0) == iota((24, 24), 1)).astype(F32)
    pick = select_velocity(64)
    viscous_diag = jnp.sum(
        dot_nt(pick, viscous_ref[...] * eye, precision=EXACT), axis=1, keepdims=True
    )
    brink_diag = jnp.sum(dot_nt(pick, brink_ref[...] * eye, precision=EXACT), axis=1, keepdims=True)

    def diagonal(q, qc, e):
        start = (q * 2 + qc) * 8
        value = (
            viscous_diag[start : start + 8] + brink_diag[start : start + 8] * brinkman_ref[e : e + 1, :]
        )
        return jnp.where(inside, value, 0.0)

    owned, diag = [], []
    for r in range(ROWS):
        at = slice(r * LANES, (r + 1) * LANES)
        weight = 1.0 - jnp.broadcast_to(tables[64 + r : 65 + r], (8, LANES))
        load = jnp.concatenate([load_ref[0, 0, 0, :, at], load_ref[0, 0, 1, :, at]], axis=0)
        owned.append(load * weight)
        diag.append(node_row(r, diagonal))
    put_rows(own_ref, owned)
    put_rows(own_ref, diag, 8)
    gather_slots([owned, diag], lane_ref, row_ref, send_refs)
    for r in range(ROWS):
        at = slice(r * LANES, (r + 1) * LANES)
        hi_ref[:, at] = jnp.broadcast_to(tables[r : r + 1].astype(jnp.int32), (8, LANES))
        lo_ref[:, at] = jnp.broadcast_to(tables[32 + r : 33 + r].astype(jnp.int32), (8, LANES))
        weight_ref[:, at] = 1.0 - jnp.broadcast_to(tables[64 + r : 65 + r], (8, LANES))


def matrix_kernel(
    viscous_ref,
    brink_ref,
    coupling_ref,
    stab_ref,
    divergence_ref,
    schur_ref,
    gradient_ref,
    image_ref,
    bias_ref,
):
    velocity, velocity_in = select_velocity(64), select_velocity(192)
    pressure, pressure_in = select_field(64, 3), select_field(192, 3)
    same = (iota((64, 192), 0) // 4) % 2 == (iota((64, 192), 1) // 4) % 2
    coarse = iota((64, 192), 1) < 128
    from_velocity = iota((64, 192), 1) % 4 != 3
    to_velocity = iota((64, 192), 0) % 4 != 3

    def placed(rows, whole, cols, first=dot_nn):
        high = whole.astype(BF16).astype(F32)
        found = []
        for piece in (high, (whole - high).astype(BF16).astype(F32)):
            found.append(dot_nt(first(rows, piece), cols))
        return jnp.where(same, jnp.where(coarse, found[0], found[1]), 0.0)

    coupling = coupling_ref[...]
    down = placed(pressure, coupling, velocity_in)
    up = placed(velocity, coupling, pressure_in, dot_nt)
    divergence_ref[...] = down.astype(BF16)
    gradient_ref[...] = up.astype(BF16)
    schur_ref[...] = placed(select_field(64, 0), coupling * coupling, velocity_in).astype(BF16)
    viscous = placed(velocity, viscous_ref[...], velocity_in, dot_nt)
    stab = placed(pressure, stab_ref[...], pressure_in, dot_nt)
    image_ref[0:64, :] = jnp.where(
        to_velocity,
        jnp.where(from_velocity, viscous, up),
        jnp.where(from_velocity, down, -stab),
    ).astype(BF16)
    image_ref[64:128, :] = placed(velocity, brink_ref[...], velocity_in, dot_nt).astype(BF16)
    eye = (iota((8, 8), 0) == iota((8, 8), 1)).astype(F32)
    bias = jnp.sum(
        dot_nt(select_field(64, 0), stab_ref[...] * eye, precision=EXACT), axis=1, keepdims=True
    )
    bias_ref[...] = jnp.where(iota((64, LANES), 1) < EZ, bias, 0.0)


def diagonal_kernel(
    own_ref,
    lane_ref,
    row_ref,
    hi_ref,
    lo_ref,
    divergence_ref,
    schur_ref,
    bias_ref,
    *refs,
):
    recv_refs, (vector_ref, inverse_ref, part_ref) = refs[:5], refs[5:8]
    send_refs = refs[8:13]
    x_ref, o_ref = refs[13:]
    diag = scattered(rows_of(own_ref, 8), hi_ref, lo_ref, recv_refs, 8)
    inverse = [jnp.where(velocity_rows(), 1.0 / value, 0.0) for value in diag]
    stage(inverse, x_ref)
    put_rows(inverse_ref, inverse)
    o_ref[...] = dot_nn(schur_ref[...], x_ref[...])
    vector = scattered(rows_of(own_ref), hi_ref, lo_ref, recv_refs)
    put_rows(vector_ref, vector)
    stage([value * row_of(inverse_ref, r) for r, value in enumerate(vector)], x_ref)
    o_ref[...] += dot_nn(divergence_ref[...], x_ref[...])
    output = output_corner(o_ref)

    def with_bias(q, qc, e):
        start = (q * 2 + qc) * 8
        return output(q, qc, e) + bias_ref[start : start + 8, :]

    finish([node_row(r, with_bias) for r in range(ROWS)], part_ref, lane_ref, row_ref, send_refs)


def finish(part, part_ref, lane_ref, row_ref, send_refs):
    put_rows(part_ref, part)
    gather_slots([part], lane_ref, row_ref, send_refs)


def divergence_kernel(
    step_ref, part_ref, inverse_ref, lane_ref, row_ref, hi_ref, lo_ref, divergence_ref, *refs
):
    recv_refs, (vector_ref, out_ref) = refs[:5], refs[5:7]
    send_refs = refs[7:12]
    x_ref, o_ref = refs[12:]
    put_rows(vector_ref, scattered(rows_of(part_ref), hi_ref, lo_ref, recv_refs))

    @pl.when(step_ref[0] < KRYLOV - 1)
    def _():
        inverse = rows_of(inverse_ref)
        stage([value * inverse[r] for r, value in enumerate(rows_of(vector_ref))], x_ref)
        o_ref[...] = dot_nn(divergence_ref[...], x_ref[...])
        output = output_corner(o_ref)
        finish([node_row(r, output) for r in range(ROWS)], out_ref, lane_ref, row_ref, send_refs)


def gradient_kernel(
    step_ref,
    part_ref,
    vector_ref,
    old_schur_ref,
    lane_ref,
    row_ref,
    hi_ref,
    lo_ref,
    gradient_ref,
    *refs,
):
    recv_refs, (schur_ref, pressure_ref, out_ref) = refs[:5], refs[5:8]
    send_refs = refs[8:13]
    x_ref, o_ref = refs[13:]
    first = jnp.full((8, LANES), step_ref[0]) == 0
    summed = scattered(rows_of(part_ref), hi_ref, lo_ref, recv_refs)
    old = rows_of(old_schur_ref)
    schur = [
        jnp.where(
            velocity_rows(), 0.0, jnp.where(first, 1.0 / pltpu.roll(summed[r], 3, 0), old[r])
        )
        for r in range(ROWS)
    ]
    vector = rows_of(vector_ref)
    pressure = [(summed[r] - vector[r]) * schur[r] for r in range(ROWS)]
    stage(pressure, x_ref)
    put_rows(pressure_ref, pressure)
    put_rows(schur_ref, schur)
    o_ref[...] = dot_nn(gradient_ref[...], x_ref[...])
    output = output_corner(o_ref)
    finish([node_row(r, output) for r in range(ROWS)], out_ref, lane_ref, row_ref, send_refs)


def image_kernel(
    part_ref,
    vector_ref,
    pressure_ref,
    inverse_ref,
    brinkman_ref,
    lane_ref,
    row_ref,
    hi_ref,
    lo_ref,
    image_ref,
    *refs,
):
    recv_refs, (direction_ref, out_ref) = refs[:5], refs[5:7]
    send_refs = refs[7:12]
    x_ref, o_ref = refs[12:]
    gradient = scattered(rows_of(part_ref), hi_ref, lo_ref, recv_refs)
    direction = [
        (row_of(vector_ref, r) - gradient[r]) * row_of(inverse_ref, r) + row_of(pressure_ref, r)
        for r in range(ROWS)
    ]
    stage(direction, x_ref)
    put_rows(direction_ref, direction)
    o_ref[...] = dot_nn(image_ref[...], x_ref[...])
    viscous, brink = output_corner(o_ref), output_corner(o_ref, 64)

    def corner_value(q, qc, e):
        return viscous(q, qc, e) + brink(q, qc, e) * brinkman_ref[e : e + 1, :]

    part = []
    for r in range(ROWS):
        share = jnp.where(row_of(hi_ref, r) > 0, 0.5 * SHIFT, SHIFT)
        part.append(node_row(r, corner_value) - share * row_of(vector_ref, r))
    finish(part, out_ref, lane_ref, row_ref, send_refs)


def largest(ref):
    top = jnp.abs(row_of(ref, 0))
    for r in range(1, ROWS):
        top = jnp.maximum(top, jnp.abs(row_of(ref, r)))
    top = jnp.max(top, axis=1, keepdims=True)
    return jnp.where(top > 0.0, top, 1.0)


def gram_kernel(early_ref, last_ref, weight_ref, out_ref):
    vectors = [early_ref.at[i] for i in range(KRYLOV)] + [last_ref]
    scales = [largest(vector) for vector in vectors]
    inverse = [1.0 / scale for scale in scales]
    totals = {pair: jnp.zeros((8, LANES), F32) for pair in PAIRS}
    for r in range(ROWS):
        rows = [row_of(vector, r) * inverse[i] for i, vector in enumerate(vectors)]
        weight = row_of(weight_ref, r)
        weighted = [value * weight for value in rows]
        for i, j in PAIRS:
            totals[i, j] = totals[i, j] + weighted[i] * rows[j]
    lane = iota((8, LANES), 1)
    values = [jnp.zeros((8, LANES), F32)] + [jnp.ones((8, LANES), F32)] * 2
    for at, (i, j) in enumerate(PAIRS):
        entries = jnp.sum(totals[i, j], axis=1, keepdims=True), scales[i], scales[j]
        values = [jnp.where(lane == at, new, old) for new, old in zip(entries, values)]
    for k, value in enumerate(values):
        out_ref[8 * k : 8 * k + 8, :] = value


def merged(items):
    tops = []
    for side in (1, 2):
        top = items[0][side]
        for item in items[1:]:
            top = jnp.maximum(top, item[side])
        tops.append(top)
    inverse = [1.0 / top for top in tops]
    total = None
    for dots, left, right in items:
        value = dots * (left * inverse[0]) * (right * inverse[1])
        total = value if total is None else total + value
    return total, tops[0], tops[1]


def planes(ref):
    return ref[0:8, :], ref[8:16, :], ref[16:24, :]


def merge_kernel(*refs):
    for k, value in enumerate(merged([planes(ref) for ref in refs[:-1]])):
        refs[-1][8 * k : 8 * (k + 1), :] = value


def solve_kernel(own_ref, other_ref, direction_ref, solution_ref, coefficient_ref):
    whole = merged([planes(own_ref), planes(other_ref)])
    cases = []
    for case in range(CASES):
        channels = [
            tuple(plane[4 * case + f : 4 * case + f + 1, :] for plane in whole) for f in range(4)
        ]
        cases.append(merged(channels))
    dots, left, right = [jnp.concatenate([item[k] for item in cases], axis=0) for k in range(3)]
    lane = iota((CASES, LANES), 1)

    def entry(values, pair):
        at = PAIRS.index(pair)
        return jnp.sum(jnp.where(lane == at, values, 0.0), axis=1, keepdims=True)

    size = KRYLOV + 1
    scale = [entry(right, (j, j)) for j in range(size)]
    upper = {}
    for j in range(size):
        for i in range(j + 1):
            value = entry(dots, (i, j))
            for k in range(i):
                value = value - upper[k, i] * upper[k, j]
            upper[i, j] = jnp.sqrt(value) if i == j else value / upper[i, i]
    step = [scale[j + 1] / scale[j] for j in range(KRYLOV)]
    h = {}
    for i in range(size):
        line = []
        for j in range(KRYLOV):
            value = jnp.zeros_like(scale[0])
            if i <= j:
                value = value + SHIFT * upper[i, j]
            if i <= j + 1:
                value = value + upper[i, j + 1] * step[j]
            line.append(value)
        for j in range(KRYLOV):
            value = line[j]
            for k in range(j):
                value = value - h[i, k] * upper[k, j]
            h[i, j] = value / upper[j, j] if i <= j + 1 else jnp.zeros_like(scale[0])
    beta = scale[0] * upper[0, 0]
    target = [beta * h[0, j] for j in range(KRYLOV)]
    factor = {}
    for j in range(KRYLOV):
        for i in range(j, KRYLOV):
            value = sum(h[m, i] * h[m, j] for m in range(size))
            for k in range(j):
                value = value - factor[i, k] * factor[j, k]
            factor[i, j] = jnp.sqrt(value) if i == j else value / factor[j, j]
    middle = []
    for i in range(KRYLOV):
        rest = target[i]
        for k in range(i):
            rest = rest - factor[i, k] * middle[k]
        middle.append(rest / factor[i, i])
    y = [None] * KRYLOV
    for i in reversed(range(KRYLOV)):
        rest = middle[i]
        for k in range(i + 1, KRYLOV):
            rest = rest - factor[k, i] * y[k]
        y[i] = rest / factor[i, i]
    for i in range(KRYLOV):
        coefficient_ref[:, i : i + 1] = y[i]
    c = [None] * KRYLOV
    for i in reversed(range(KRYLOV)):
        rest = y[i]
        for k in range(i + 1, KRYLOV):
            rest = rest - upper[i, k] * c[k]
        c[i] = rest / upper[i, i]
    c = [c[i] / scale[i] for i in range(KRYLOV)]
    for case in range(CASES):
        factors = [jnp.broadcast_to(c[i][case : case + 1], (4, LANES)) for i in range(KRYLOV)]
        for r in range(ROWS):
            at = slice(r * LANES, (r + 1) * LANES)
            span = slice(4 * case, 4 * case + 4)
            value = factors[0] * direction_ref[0, span, at]
            for i in range(1, KRYLOV):
                value = value + factors[i] * direction_ref[i, span, at]
            solution_ref[0, 0, case, :, at] = value


def field(rows=8, cols=NODES, kind=F32):
    return jax.ShapeDtypeStruct((rows, cols), kind)


def sends(rows=8):
    return [field(rows, size) for size in SIZES]


STENCIL = [
    pltpu.VMEM((192, ELEM_ROWS * LANES), BF16),
]


def stencil(rows=64):
    return STENCIL + [pltpu.VMEM((rows, ELEM_ROWS * LANES), F32)]


def call(kernel, outs, args, name, smem=(), scratch=(), cost=2000):
    return pl.pallas_call(
        kernel,
        out_shape=outs,
        in_specs=[SMEM if i in smem else VMEM for i in range(len(args))],
        out_specs=jax.tree.map(lambda _: VMEM, outs),
        scratch_shapes=scratch,
        name=name,
        compiler_params=pltpu.CompilerParams(vmem_limit_bytes=8 << 20),
        cost_estimate=pl.CostEstimate(flops=cost * 1000, bytes_accessed=cost * 1000, transcendentals=0),
    )(*args)


def exclusive(count, masks):
    return [[(i, i ^ mask) for i in range(count)] for mask in masks]


def exchange(buffers):
    subs = exclusive(lax.axis_size("sub"), (1, 2, 4))
    slabs = lax.axis_size("slab")
    first = [(i, i ^ 1) for i in range(slabs)]
    second = [(i, ((i + 1) ^ 1) - 1 if 0 < i < slabs - 1 else slabs - 1 - i) for i in range(slabs)]
    routes = [("sub", route) for route in subs] + [("slab", first), ("slab", second)]
    received = [None] * len(buffers)
    for k in (2, 3, 4, 1, 0):
        received[k] = lax.ppermute(buffers[k], *routes[k])
    return received


def swapped(item, axis, mask):
    return lax.ppermute(item, axis, exclusive(lax.axis_size(axis), (mask,))[0])


def per_device(
    adjoint_load,
    design,
    viscous_block,
    brinkman_block,
    coupling,
    stabilization,
    neighbours,
    iface_nodes,
    iface_count,
    face_nodes,
    owner_ids,
):
    slots = GROUPS * LANES
    outs = call(
        setup_kernel,
        [
            field(16),
            field(8, slots, jnp.int32),
            field(8, slots, jnp.int32),
            field(kind=jnp.int32),
            field(kind=jnp.int32),
            field(),
            field(ELEM_ROWS, LANES),
        ]
        + sends(16),
        (
            iface_count,
            neighbours,
            adjoint_load,
            design.reshape(1, ELEM_ROWS * EZ),
            viscous_block,
            brinkman_block,
            iface_nodes.reshape(-1, LANES),
            face_nodes.reshape(-1, LANES),
            owner_ids.reshape(-1, LANES),
        ),
        "setup",
        smem=(0, 1),
    )
    own, lanes, rows, hi, lo, weights, brinkman = outs[:7]
    received = exchange(outs[7:])
    divergence_map, schur_map, gradient_map, image_map, bias = call(
        matrix_kernel,
        [field(64, 192, BF16)] * 3 + [field(128, 192, BF16), field(64, LANES)],
        (viscous_block, brinkman_block, coupling, stabilization),
        "matrices",
    )
    tables = (lanes, rows, hi, lo)
    outs = call(
        diagonal_kernel,
        [field(), field(), field()] + sends(),
        (own, *tables, divergence_map, schur_map, bias, *received),
        "diagonal",
        scratch=stencil(),
    )
    vector, inverse, part = outs[:3]
    sent = tuple(outs[3:])

    def krylov_step(step, carry):
        vector, part, schur, basis, directions, sent = carry
        basis = lax.dynamic_update_index_in_dim(basis, vector, step, 0)
        at = jnp.full((1,), step, jnp.int32)
        received = exchange(sent)
        schur, pressure, part, *sent = call(
            gradient_kernel,
            [field(), field(), field()] + sends(),
            (at, part, vector, schur, *tables, gradient_map, *received),
            "gradient",
            smem=(0,),
            scratch=stencil(),
        )
        received = exchange(sent)
        direction, part, *sent = call(
            image_kernel,
            [field(), field()] + sends(),
            (part, vector, pressure, inverse, brinkman, *tables, image_map, *received),
            "image",
            scratch=stencil(128),
        )
        directions = lax.dynamic_update_index_in_dim(directions, direction, step, 0)
        received = exchange(sent)
        vector, part, *sent = call(
            divergence_kernel,
            [field(), field()] + sends(),
            (at, part, inverse, *tables, divergence_map, *received),
            "divergence",
            smem=(0,),
            scratch=stencil(),
        )
        return vector, part, schur, basis, directions, tuple(sent)

    empty = jnp.zeros((KRYLOV, 8, NODES), F32)
    vector, _, _, basis, directions, _ = lax.fori_loop(
        0, KRYLOV, krylov_step, (vector, part, inverse, empty, empty, sent)
    )
    item = call(gram_kernel, field(24, LANES), (basis, vector, weights), "gram")
    hops = [("sub", 1 << bit) for bit in range(6)] + [("slab", 1), ("slab", 2)]
    for axis, mask in hops[:-1]:
        item = call(
            merge_kernel, field(24, LANES), (item, swapped(item, axis, mask)), "merge", cost=10
        )
    return tuple(
        call(
            solve_kernel,
            [
                jax.ShapeDtypeStruct((1, 1, CASES, 4, NODES), F32),
                jax.ShapeDtypeStruct((CASES, KRYLOV), F32),
            ],
            (item, swapped(item, *hops[-1]), directions),
            "solve",
        )
    )


def solution(mesh):
    placed = (
        P("slab", "sub", None, None, None),
        P("slab", "sub", None),
        P(),
        P(),
        P(),
        P(),
        P("slab", "sub", None),
        P("slab", "sub", None, None),
        P("slab", "sub", None),
        P("slab", "sub", None, None),
        P("slab", "sub", None, None),
    )
    return jax.shard_map(
        per_device,
        mesh=mesh,
        in_specs=placed,
        out_specs=(P("slab", "sub", None, None, None), P()),
        check_vma=False,
    )
```
